32 devices in a mesh: fsdp: 2 (over x), ctx: 4 (over y, core), tp: 4 (over z).
Axes of the slice: x: 2, y: 2, z: 4, core: 2. Of those that a mesh axis runs over, the one named last changes fastest.
Arguments:
- tokens: bfloat16 [8, 512, 768], P(('fsdp', 'tp'), 'ctx'), may hold values from -6 to 6
- seg_ids: int32 [8, 512], P(('fsdp', 'tp')), may hold values from 0 to 2, never falling along the last dimension, each value on 1 to 384 neighbouring positions
- routes: int32 [8, 512, 2], P(('fsdp', 'tp'), 'ctx'), may hold values from 0 to 3, all different within a row; in each aligned block of 128 rows (0 to 127, 128 to 255, ..., all dimensions but the last counted through in order) at most 80 rows name the same one
- norm_attn: bfloat16 [768], P('fsdp'), may hold values from 0.5 to 1.5
- weight_qkv: bfloat16 [768, 2304], P('fsdp'), may hold values from -0.21875 to 0.21875
- weight_proj: bfloat16 [768, 768], P(None, 'fsdp'), may hold values from -0.875 to 0.875
- rel_table: float32 [12, 32], replicated, may hold values from -4 to 4
- norm_ffn: bfloat16 [768], P('fsdp'), may hold values from 0.5 to 1.5
- weight_router: bfloat16 [768, 4], P('fsdp'), may hold values from -0.21875 to 0.21875
- expert_up: bfloat16 [4, 768, 3072], P(None, 'fsdp', ('ctx', 'tp')), may hold values from -0.21875 to 0.21875
- expert_down: bfloat16 [4, 3072, 768], P(None, ('ctx', 'tp'), 'fsdp'), may hold values from -0.109375 to 0.109375
- cotangent: bfloat16 [8, 512, 768], P(('fsdp', 'tp'), 'ctx'), may hold values from -6 to 6
Outputs:
- output: bfloat16 [8, 512, 768], P(('fsdp', 'tp'), 'ctx')
- grad_tokens: float32 [8, 512, 768], P(('fsdp', 'tp'), 'ctx')
- grad_norm_attn: float32 [768], P('fsdp')
- grad_weight_qkv: float32 [768, 2304], P('fsdp')
- grad_weight_proj: float32 [768, 768], P(None, 'fsdp')
- grad_rel_table: float32 [12, 32], replicated
- grad_norm_ffn: float32 [768], P('fsdp')
- grad_weight_router: float32 [768, 4], P('fsdp')
- grad_expert_up: float32 [4, 768, 3072], P(None, 'fsdp', ('ctx', 'tp'))
- grad_expert_down: float32 [4, 3072, 768], P(None, ('ctx', 'tp'), 'fsdp')
The draws below stay inside these ranges and needn't reach their ends.
Inputs may be any that keep to these rules, and one draw needn't show every extreme that they name: `seg_ids`: each group's 512 positions fall into at most 3 sequences whose numbers never fall along the positions; the longest has exactly 384 positions. `routes`: each token names two different experts. In each aligned block of 128 rows (the rows of one device) no expert is named more than 80 times, and in every draw some expert is named exactly 80 times in some block.
All inputs are finite; a program needn't handle non-finite values.
Results may differ from the reference program's by a relative error of at most 0.012.
Values may be sent and summed in bfloat16 or wider, within the bound.
A program may use at most 192 MiB of HBM per device.

```python
import math
from functools import partial
import jax
import jax.numpy as jnp
import numpy as np
from jax import lax

D = 768
HEADS = 12
HD = 64
FF = 3072
EXPERTS = 4
TOP = 2
BUCKETS = 32
MAX_DISTANCE = 128
SEGS = 3
TOK_DEV = 128
MOST = 80
GROUP_LEN = 512
SEG_MOST = 384
GROUPS = 8


def spiked(entries, stream_key, source, target, parts, factor):
    def block_of(dim):
        return (jnp.arange(entries.shape[dim]) // (entries.shape[dim] // parts)).reshape((-1,) + (1,) * (entries.ndim - 1 - dim))

    first = jax.random.permutation(stream_key, parts)[block_of(target)]
    second = (block_of(target) + parts // 2) % parts
    return jnp.where((block_of(source) == first) | (block_of(source) == second), factor * entries, entries)


def shard_levels(rng, shape, cuts, smallest, largest):
    def one(dim, parts):
        steps = jax.random.uniform(jax.random.fold_in(jax.random.fold_in(rng, 6), dim), (parts,), jnp.float32, smallest / len(cuts), largest / len(cuts))
        return jnp.repeat(jnp.exp(steps), shape[dim] // parts).reshape((-1,) + (1,) * (len(shape) - dim - 1))

    level = one(*cuts[0])
    for cut in cuts[1:]:
        level = level * one(*cut)
    return level


def split_up(number_of, total, most, skew):
    portions = [(1 << 20) // math.isqrt(grade ** skew) + 1 for grade in range(2, number_of + 1)]
    spare, counts = total - most - (number_of - 1), [1] * (number_of - 1)
    while spare > 0:
        free = [i for i in range(number_of - 1) if counts[i] < most]
        whole, left = sum([portions[i] for i in free]), spare
        for i in free:
            extra = min(most - counts[i], max(1, left * portions[i] // whole), spare)
            counts[i] = counts[i] + extra
            spare = spare - extra
    return np.array([most] + counts)


def uneven(rng, count, total, bound, skew):
    if count == 2:
        one = jax.random.randint(rng, (), max(1, total - bound), min(bound, total - 1) + 1)
        return jnp.stack([one, total - one])
    tallies = jnp.asarray(split_up(count, total, bound, skew), jnp.int32)
    pairs = (count - 1) // 2
    donor, receiver = tallies[1:1 + 2 * pairs:2], tallies[2:2 + 2 * pairs:2]
    margin = jnp.minimum(donor - 1, bound - receiver)
    shifted = jax.random.randint(jax.random.fold_in(rng, 1), (pairs,), 0, 1 << 20) % (margin + 1)
    tallies = tallies.at[1:1 + 2 * pairs:2].set(donor - shifted).at[2:2 + 2 * pairs:2].set(receiver + shifted)
    return tallies[jax.random.permutation(jax.random.fold_in(rng, 2), count)]


def assign_block(stream_key, own, number, rows, amount, top, bound, skew):
    sequence = jax.random.permutation(stream_key, amount)
    heavy_load, usual = shares(amount, rows * top, bound, skew, True), shares(amount, rows * top, bound, skew, False)
    places = jnp.arange(amount)

    def named(lengths, rotation):
        used = int((lengths > 0).sum())
        fixed = max(1, used // 4)
        passed = fixed + (places - fixed + rotation * (used - fixed)) % max(1, amount - fixed)
        return jnp.zeros((amount,), jnp.int32).at[sequence[jnp.where(places < fixed, places, passed)]].set(jnp.asarray(lengths, jnp.int32))

    lengths = jnp.where(number % 4 == 0, named(heavy_load, number // 4), named(usual, number - number // 4 - 1))
    mixed = jax.random.permutation(jax.random.fold_in(own, 3), amount)
    donor, taker = mixed[0:amount // 2 * 2:2], mixed[1:amount // 2 * 2:2]
    margin = jnp.minimum(lengths[donor] - 1, bound - lengths[taker]) // 2
    margin = jnp.where((donor == sequence[0]) | (taker == sequence[0]) | (lengths[taker] == 0), 0, jnp.maximum(margin, 0))
    passed = jax.random.randint(jax.random.fold_in(own, 4), (amount // 2,), 0, 1 << 20) % (margin + 1)
    lengths = lengths.at[donor].add(-passed).at[taker].add(passed)
    items = jnp.searchsorted(jnp.cumsum(lengths), jnp.arange(rows * top), side="right").astype(jnp.int32)
    grid = items.reshape(top, rows).T
    grid = grid[jax.random.permutation(jax.random.fold_in(own, 1), rows)]
    rotation = jax.random.randint(jax.random.fold_in(own, 2), (rows, 1), 0, top)
    return jnp.take_along_axis(grid, (jnp.arange(top)[None, :] + rotation) % top, axis=1)


def shares(count, total, bound, skew, full):
    loads = [(1 << 20) // math.isqrt(rank ** skew) + 1 for rank in range(1, count + 1)]
    largest = bound if full else min(bound, max(-(-total // count), total * loads[0] // sum(loads)))
    least = 1 if total - largest >= count - 1 else 0
    given, spare = [largest] + [least] * (count - 1), total - largest - least * (count - 1)
    while spare > 0:
        candidates = [i for i in range(1, count) if given[i] < largest] or [i for i in range(1, count) if given[i] < bound]
        whole, budget = sum([loads[i] for i in candidates]), spare
        for i in candidates:
            extra = min(bound - given[i], max(1, budget * loads[i] // whole), spare)
            given[i] = given[i] + extra
            spare = spare - extra
    return np.array(given)


def noise(stream_key, dims, deviation, limit, split=(), kind=jnp.bfloat16):
    level = shard_levels(stream_key, dims, split, -0.22, 0.18) if split else 1.0
    values = jax.random.normal(stream_key, dims, jnp.float32) * deviation * level
    return jnp.minimum(jnp.maximum(values, -limit), limit).astype(kind)


def gaussian_with(key, extent, deviation, bound, split, heavy, held_as=jnp.bfloat16):
    entries = deviation * jax.random.normal(key, extent, jnp.float32)
    if split:
        entries = entries * shard_levels(key, extent, split, -0.22, 0.18)
    return jnp.clip(spiked(entries, jax.random.fold_in(key, 3), *heavy), -bound, bound).astype(held_as)


def setup_inputs(seed: int = 0) -> dict:
    keys = jax.random.split(jax.random.key(seed), 13)
    tokens = noise(keys[0], (GROUPS, GROUP_LEN, D), 1.0, 6.0, ((0, 8), (1, 4)))
    seg_ids = jax.vmap(lambda own: jnp.searchsorted(jnp.cumsum(uneven(own, SEGS, GROUP_LEN, SEG_MOST, 2)), jnp.arange(GROUP_LEN), side="right"))(jax.random.split(keys[1], GROUPS)).reshape((GROUPS, GROUP_LEN)).astype(jnp.int32)
    routes_keys = jax.random.split(jax.random.fold_in(keys[2], 1), GROUPS * GROUP_LEN // TOK_DEV)
    routes_turns = jax.random.permutation(jax.random.fold_in(keys[2], 3), GROUPS * GROUP_LEN // TOK_DEV)
    routes = jax.vmap(lambda own, number: assign_block(jax.random.fold_in(keys[2], 2), own, number, TOK_DEV, EXPERTS, TOP, MOST, 1))(routes_keys, routes_turns).reshape((GROUPS, GROUP_LEN, TOP))
    norm_attn = jnp.clip(1.0 + 0.1 * jax.random.normal(keys[3], (D,), jnp.float32), 0.5, 1.5).astype(jnp.bfloat16)
    weight_qkv = noise(keys[4], (D, 3 * D), D ** -0.5, 0.21875, ((0, 2),))
    weight_proj = noise(keys[5], (D, D), (D // 16) ** -0.5, 0.875, ((1, 2),))
    rel_table = noise(keys[6], (HEADS, BUCKETS), 1.0, 4.0, (), jnp.float32)
    norm_ffn = jnp.clip(1.0 + 0.1 * jax.random.normal(keys[7], (D,), jnp.float32), 0.5, 1.5).astype(jnp.bfloat16)
    weight_router = noise(keys[8], (D, EXPERTS), D ** -0.5, 0.21875, ((0, 2),))
    expert_up = noise(keys[9], (EXPERTS, D, FF), D ** -0.5, 0.21875, ((1, 2), (2, 16)))
    expert_down = noise(keys[10], (EXPERTS, FF, D), FF ** -0.5, 0.109375, ((1, 16), (2, 2)))
    cotangent = gaussian_with(keys[11], (GROUPS, GROUP_LEN, D), 1.0, 6.0, ((0, 8), (1, 4)), (0, 2, 8, 2.0))
    return {"tokens": tokens, "seg_ids": seg_ids, "routes": routes, "norm_attn": norm_attn, "weight_qkv": weight_qkv, "weight_proj": weight_proj, "rel_table": rel_table, "norm_ffn": norm_ffn, "weight_router": weight_router, "expert_up": expert_up, "expert_down": expert_down, "cotangent": cotangent}


EPSILON = 1e-06
MASK_FILL = -1e+30

@jax.custom_vjp
def low(v):
    return lax.optimization_barrier(v.astype(jnp.bfloat16)).astype(jnp.float32)

@jax.custom_vjp
def low_back(v):
    return v

def low_keep(v):
    return (low(v), None)

def low_pass(kept, grad):
    return (grad,)

def back_keep(v):
    return (v, None)

def back_low(kept, grad):
    return (low(grad),)
low.defvjp(low_keep, low_pass)
low_back.defvjp(back_keep, back_low)

def bucket_bounds(buckets, far_reach):
    exact_count = buckets // 2
    bounds = []
    for number in range(1, buckets):
        if number <= exact_count:
            bounds.append(number)
        else:
            exponent = (number - exact_count) / (buckets - exact_count)
            bounds.append(int(np.ceil(exact_count * (far_reach / exact_count) ** exponent)))
    return np.array(bounds, dtype=np.int32)

def slot_tables(route_ids, experts, capacity):
    flat_ids = route_ids.reshape(-1)
    assignments = flat_ids.shape[0]
    member = (flat_ids[:, None] == jnp.arange(experts, dtype=jnp.int32)[None, :]).astype(jnp.int32)
    before = jnp.cumsum(member, axis=0) - member
    slot_index = lax.optimization_barrier(jnp.sum(before * member, axis=1))
    position = slot_index * experts + flat_ids
    filler = jnp.full((capacity * experts,), assignments, jnp.int32).at[position].set(jnp.arange(assignments, dtype=jnp.int32))
    return (position, filler)

def take_rows(table_rows, indices):
    return table_rows[indices]

def rms_norm(values, gain):
    return values * lax.rsqrt(lax.optimization_barrier(jnp.mean(values * values, axis=-1, keepdims=True)) + EPSILON) * gain

def forward(tokens, norm_attn, weight_qkv, weight_proj, rel_table, norm_ffn, weight_router, expert_up, expert_down, seg_ids, routes):
    highest = lax.Precision.HIGHEST
    token_total = GROUPS * GROUP_LEN
    inputs = tokens.reshape(token_total, D)
    normed_one = low(rms_norm(inputs, norm_attn))
    projected = low_back(low(jnp.dot(normed_one, weight_qkv, precision=highest)))
    by_group = projected.reshape(GROUPS, GROUP_LEN, 3, HEADS, HD)
    positions = jnp.arange(GROUP_LEN, dtype=jnp.int32)
    distance = jnp.maximum(positions[:, None] - positions[None, :], 0)
    bounds = jnp.asarray(bucket_bounds(BUCKETS, MAX_DISTANCE))
    which_bucket = lax.optimization_barrier(jnp.sum((distance[:, :, None] >= bounds[None, None, :]).astype(jnp.int32), axis=2))

    def one_group(pieces):
        group_qkv, segment = pieces
        products = jnp.einsum('qhd,khd->hqk', group_qkv[:, 0], group_qkv[:, 1], precision=highest)
        scores = low_back(products * HD ** (-0.5) + rel_table[:, which_bucket])
        allowed = (segment[:, None] == segment[None, :]) & (positions[:, None] >= positions[None, :])
        probs = low(jax.nn.softmax(jnp.where(allowed[None], scores, MASK_FILL), axis=-1))
        return low_back(low(jnp.einsum('hqk,khd->qhd', probs, group_qkv[:, 2], precision=highest)))
    attended = lax.map(jax.checkpoint(one_group), (by_group, seg_ids))
    mixed_heads = attended.reshape(token_total, D)
    attention = low_back(jnp.dot(mixed_heads, weight_proj, precision=highest))
    middle = inputs + attention
    normed_two = low(rms_norm(middle, norm_ffn))
    logits = jnp.dot(normed_two, weight_router, precision=highest)
    route_rows = routes.reshape(token_total, TOP)
    gate_weights = jax.nn.softmax(jnp.take_along_axis(logits, route_rows, axis=1), axis=-1)
    block_count = token_total // TOK_DEV
    position, filler = jax.vmap(partial(slot_tables, experts=EXPERTS, capacity=MOST))(routes.reshape(block_count, TOK_DEV, TOP))
    offsets = (jnp.arange(block_count, dtype=jnp.int32) * TOK_DEV)[:, None]
    owner = jnp.where(filler < 2 * TOK_DEV, offsets + filler // 2, token_total)
    padded_rows = jnp.concatenate([normed_two, jnp.zeros((1, D), jnp.float32)], axis=0)
    dispatched = padded_rows[owner].reshape(block_count * MOST, EXPERTS, D)
    by_expert = jnp.transpose(dispatched, (1, 0, 2))

    def one_expert(pieces):
        expert_rows, up_matrix, down_matrix = pieces
        pre_act = low_back(jnp.dot(expert_rows, up_matrix, precision=highest))
        activated = low(jax.nn.gelu(pre_act))
        return low_back(jnp.dot(activated, down_matrix, precision=highest))
    expert_result = lax.map(jax.checkpoint(one_expert), (by_expert, expert_up, expert_down))
    slot_result = jnp.transpose(expert_result, (1, 0, 2)).reshape(block_count, MOST * EXPERTS, D)
    per_choice = jax.vmap(take_rows)(slot_result, position).reshape(token_total, TOP, D)
    result = middle + lax.optimization_barrier(jnp.sum(gate_weights[:, :, None] * per_choice, axis=1))
    return result.reshape(GROUPS, GROUP_LEN, D)

def reference(tokens, seg_ids, routes, norm_attn, weight_qkv, weight_proj, rel_table, norm_ffn, weight_router, expert_up, expert_down, cotangent):
    floats = (tokens.astype(jnp.float32), norm_attn.astype(jnp.float32), weight_qkv.astype(jnp.float32), weight_proj.astype(jnp.float32), rel_table.astype(jnp.float32), norm_ffn.astype(jnp.float32), weight_router.astype(jnp.float32), expert_up.astype(jnp.float32), expert_down.astype(jnp.float32))

    def closed(*arrays):
        return forward(*arrays, seg_ids, routes)
    result, pullback = jax.vjp(closed, *floats)
    gradients = pullback(cotangent.astype(jnp.float32))
    return (result.astype(jnp.bfloat16), gradients[0], gradients[1], gradients[2], gradients[3], gradients[4], gradients[5], gradients[6], gradients[7], gradients[8])
```

```python
import jax
import jax.numpy as jnp
import numpy as np
from jax import lax
from jax.sharding import PartitionSpec as P

BUCKETS = 32
MAX_DISTANCE = 128
EPSILON = 1e-06
MASK_FILL = -1e30
F32 = jnp.float32
BF16 = jnp.bfloat16


def bucket_bounds(buckets, far_reach):
    exact_count = buckets // 2
    bounds = []
    for number in range(1, buckets):
        if number <= exact_count:
            bounds.append(number)
        else:
            exponent = (number - exact_count) / (buckets - exact_count)
            bounds.append(int(np.ceil(exact_count * (far_reach / exact_count) ** exponent)))
    return bounds


BOUNDS = bucket_bounds(BUCKETS, MAX_DISTANCE)


def rms_scale(values):
    return lax.rsqrt(jnp.mean(values * values, axis=-1, keepdims=True) + EPSILON)


def dot(a, b, ca, cb):
    return lax.dot_general(a, b, (((ca,), (cb,)), ((), ())), preferred_element_type=F32)


def exchange_sum(part, axis, dim):
    count = lax.axis_size(axis)
    size = part.shape[dim] // count
    me = lax.axis_index(axis)
    total = lax.dynamic_slice_in_dim(part, me * size, size, dim)
    for step in range(1, count):
        target = lax.rem(me + step, count)
        piece = lax.dynamic_slice_in_dim(part, target * size, size, dim).astype(BF16)
        total = total + lax.ppermute(
            piece, axis, [(i, (i + step) % count) for i in range(count)]
        ).astype(F32)
    return total


def local(
    tokens,
    seg_ids,
    routes,
    norm_attn,
    weight_qkv,
    weight_proj,
    rel_table,
    norm_ffn,
    weight_router,
    expert_up,
    expert_down,
    cotangent,
):
    rows = tokens.shape[1]
    width = tokens.shape[2]
    heads = rel_table.shape[0]
    head_size = width // heads
    ctx_count = lax.axis_size("ctx")
    heads_here = heads // ctx_count
    hw = heads_here * head_size
    experts = expert_up.shape[0]
    units = expert_up.shape[2]
    length = seg_ids.shape[1]
    score_scale = head_size ** (-0.5)
    ctx_index = lax.axis_index("ctx")
    fsdp_index = lax.axis_index("fsdp")
    own_width = norm_attn.shape[0]
    world = ("ctx", "tp")

    token_group = lax.all_gather(tokens[0], "ctx", axis=0, tiled=True)
    small = jnp.concatenate([norm_attn[None], norm_ffn[None], weight_router.T], axis=0)
    small = lax.all_gather(small, "fsdp", axis=1, tiled=True)
    gain_one = small[0].astype(F32)
    gain_two = small[1].astype(F32)
    router_t = small[2:]
    qkv_part = jnp.concatenate(
        [
            lax.dynamic_slice_in_dim(weight_qkv, s * width + ctx_index * hw, hw, 1)
            for s in range(3)
        ],
        axis=1,
    )
    qkv_here = lax.all_gather(qkv_part, "fsdp", axis=0, tiled=True)
    proj_full = lax.all_gather(weight_proj, "fsdp", axis=1, tiled=True)
    route_all = lax.all_gather(routes[0], world, axis=0, tiled=True)
    up_t = lax.all_gather(
        jnp.swapaxes(expert_up, 1, 2).reshape(experts * units, own_width),
        "fsdp",
        axis=1,
        tiled=True,
    )
    down = lax.all_gather(
        expert_down.reshape(experts * units, own_width), "fsdp", axis=1, tiled=True
    )
    grad_all = lax.all_gather(cotangent[0], world, axis=0, tiled=True)

    block = MAX_DISTANCE
    table_here = lax.dynamic_slice_in_dim(rel_table, ctx_index * heads_here, heads_here, 0)
    offset = (
        lax.broadcasted_iota(jnp.int32, (1, block, block), 1)
        - lax.broadcasted_iota(jnp.int32, (1, block, block), 2)
    )

    def bias_block(distance):
        value = jnp.broadcast_to(table_here[:, 0][:, None, None], (heads_here, block, block))
        for number, bound in enumerate(BOUNDS, 1):
            value = jnp.where(distance >= bound, table_here[:, number][:, None, None], value)
        return value

    near = bias_block(offset)
    next_near = bias_block(offset + block)
    far = jnp.broadcast_to(table_here[:, BUCKETS - 1][:, None, None], (heads_here, block, block))
    blocks = length // block
    picks = {0: near, 1: next_near}
    bias = jnp.concatenate(
        [
            jnp.concatenate(
                [picks.get(i - j, far) for j in range(blocks)],
                axis=2,
            )
            for i in range(blocks)
        ],
        axis=1,
    )
    positions = jnp.arange(length, dtype=jnp.int32)
    segment = seg_ids[0]
    allowed = (segment[:, None] == segment[None, :]) & (positions[:, None] >= positions[None, :])
    bias = jnp.where(allowed[None], bias, MASK_FILL)

    inputs_group = token_group.astype(F32)
    normed_group = (inputs_group * rms_scale(inputs_group) * gain_one).astype(BF16)
    projected = dot(normed_group, qkv_here, 1, 0).astype(BF16)
    by_head = projected.reshape(length, 3, heads_here, head_size)
    query, key, value = by_head[:, 0], by_head[:, 1], by_head[:, 2]

    scores = (
        jnp.einsum("qhd,khd->hqk", query, key, preferred_element_type=F32) * score_scale + bias
    )
    peak = jnp.max(scores, axis=-1, keepdims=True)
    weights = jnp.exp(scores - peak)
    probs = weights / jnp.sum(weights, axis=-1, keepdims=True)
    low_probs = probs.astype(BF16)
    attended = (
        jnp.einsum("hqk,khd->qhd", low_probs, value, preferred_element_type=F32)
        .astype(BF16)
        .reshape(length, hw)
    )
    mixed = lax.all_to_all(attended, "ctx", split_axis=0, concat_axis=1, tiled=True)
    inputs = tokens[0].astype(F32)
    scale_one = rms_scale(inputs)
    middle = inputs + dot(mixed, proj_full, 1, 0)
    scale_two = rms_scale(middle)
    normed_two = (middle * scale_two * gain_two).astype(BF16)

    normed_all = lax.all_gather(normed_two, world, axis=0, tiled=True)

    def gates_of(normed, route):
        logits = dot(normed, router_t, 1, 1)
        number = lax.broadcasted_iota(jnp.int32, (1, experts), 1)
        chosen = (route[:, 0:1] == number) | (route[:, 1:2] == number)
        masked = jnp.where(chosen, logits, MASK_FILL)
        raw = jnp.where(chosen, jnp.exp(masked - jnp.max(masked, axis=1, keepdims=True)), 0.0)
        return raw / jnp.sum(raw, axis=1, keepdims=True)

    gates_all = gates_of(normed_all, route_all)
    column = lax.broadcasted_iota(jnp.int32, (1, experts * units), 1) // units
    spread = gates_all[:, 0:1]
    for e in range(1, experts):
        spread = jnp.where(column >= e, gates_all[:, e : e + 1], spread)
    pre = dot(normed_all, up_t, 1, 1)
    reach = dot(grad_all, down, 1, 1)
    act, gelu_back = jax.vjp(jax.nn.gelu, pre)
    act = act.astype(BF16).astype(F32)
    gated = (act * spread).astype(BF16)
    product = act * reach
    dots_all = jnp.stack(
        [
            jnp.sum(jnp.where(column == e, product, 0.0), axis=1)
            for e in range(experts)
        ],
        axis=0,
    )
    grad_pre = gelu_back(reach * spread)[0].astype(BF16)
    total_rows = normed_all.shape[0]
    devices = total_rows // rows
    dots_all = jnp.swapaxes(dots_all.reshape(experts, devices, rows), 0, 1)
    dots_own = lax.psum_scatter(
        dots_all.reshape(devices, experts * rows), world, scatter_dimension=0, tiled=True
    )
    gate_dots = dots_own.reshape(experts, rows).T
    grad_normed_two = lax.psum_scatter(
        dot(grad_pre, up_t, 1, 0).astype(BF16), world, scatter_dimension=0, tiled=True
    ).astype(F32)
    result = lax.psum_scatter(
        dot(gated, down, 1, 0).astype(BF16), world, scatter_dimension=0, tiled=True
    ).astype(F32)
    output = (middle + result).astype(BF16)[None]
    grad_up = exchange_sum(dot(grad_pre, normed_all, 0, 0), "fsdp", 1)
    grad_up = jnp.swapaxes(grad_up.reshape(experts, units, own_width), 1, 2)
    grad_down = exchange_sum(dot(gated, grad_all, 0, 0), "fsdp", 1)
    grad_down = grad_down.reshape(experts, units, own_width)

    grad_out = cotangent[0].astype(F32)
    gates = gates_of(normed_two, routes[0])
    grad_logits = gates * (gate_dots - jnp.sum(gates * gate_dots, axis=1, keepdims=True))
    grad_normed_two = grad_normed_two + jnp.dot(
        grad_logits, router_t.astype(F32), precision=lax.Precision.HIGHEST
    )
    grad_router = lax.dot_general(
        grad_logits,
        normed_two.astype(F32),
        (((0,), (0,)), ((), ())),
        precision=lax.Precision.HIGHEST,
    )
    weighted_two = grad_normed_two * gain_two
    grad_gain_two = jnp.sum(grad_normed_two * middle * scale_two, axis=0)
    grad_middle = (
        grad_out
        + scale_two * weighted_two
        - middle * scale_two**3 * jnp.mean(weighted_two * middle, axis=1, keepdims=True)
    )
    grad_mid_group = lax.all_gather(grad_middle.astype(BF16), "ctx", axis=0, tiled=True)

    proj_rows = lax.dynamic_slice_in_dim(proj_full, ctx_index * hw, hw, 0)
    grad_attended = dot(grad_mid_group, proj_rows, 1, 1).astype(BF16)
    grad_heads = grad_attended.reshape(length, heads_here, head_size)
    grad_value = jnp.einsum("hqk,qhd->khd", low_probs, grad_heads, preferred_element_type=F32)
    grad_probs = jnp.einsum("qhd,khd->hqk", grad_heads, value, preferred_element_type=F32)
    grad_scores = (
        probs * (grad_probs - jnp.sum(probs * grad_probs, axis=-1, keepdims=True))
    ).astype(BF16)
    grad_query = (
        jnp.einsum("hqk,khd->qhd", grad_scores, key, preferred_element_type=F32) * score_scale
    )
    grad_key = (
        jnp.einsum("hqk,qhd->khd", grad_scores, query, preferred_element_type=F32) * score_scale
    )
    grad_qkv = jnp.concatenate(
        [
            grad_query.astype(BF16).reshape(length, hw),
            grad_key.astype(BF16).reshape(length, hw),
            grad_value.astype(BF16).reshape(length, hw),
        ],
        axis=1,
    )
    grad_normed_one = exchange_sum(dot(grad_qkv, qkv_here, 1, 1), "ctx", 0)

    weight_part = jnp.concatenate(
        [dot(normed_group, grad_qkv, 0, 0), dot(grad_mid_group, attended, 0, 0)], axis=1
    )
    weight_own = lax.psum_scatter(
        weight_part.astype(BF16), ("fsdp", "tp"), scatter_dimension=0, tiled=True
    )
    weight_all = lax.all_gather(weight_own, world, axis=0, tiled=True).astype(F32)
    weight_all = weight_all.reshape(ctx_count, own_width, 4 * hw)
    grad_weight_qkv = jnp.concatenate(
        [
            weight_all[c, :, s * hw : (s + 1) * hw]
            for s in range(3)
            for c in range(ctx_count)
        ],
        axis=1,
    )
    grad_weight_proj = jnp.swapaxes(weight_all[:, :, 3 * hw :], 1, 2).reshape(width, own_width)

    def score_block(i, j):
        return grad_scores[
            :, i * block : (i + 1) * block, j * block : (j + 1) * block
        ].astype(F32)

    near_sum = sum(score_block(i, i) for i in range(blocks))
    next_sum = sum(score_block(i + 1, i) for i in range(blocks - 1))
    far_sum = sum(
        jnp.sum(score_block(i, j), axis=(1, 2)) for i in range(blocks) for j in range(i - 1)
    )
    lows = [0] + BOUNDS
    highs = BOUNDS + [2 * block]
    bucket_sums = [
        jnp.sum(jnp.where((offset >= lo) & (offset < hi), near_sum, 0.0), axis=(1, 2))
        + jnp.sum(
            jnp.where((offset + block >= lo) & (offset + block < hi), next_sum, 0.0), axis=(1, 2)
        )
        for lo, hi in zip(lows, highs)
    ]
    bucket_sums[-1] = bucket_sums[-1] + far_sum
    table_here_grad = jnp.stack(bucket_sums, axis=1)
    table_term = lax.dynamic_update_slice_in_dim(
        jnp.zeros((heads, BUCKETS), F32), table_here_grad, ctx_index * heads_here, 0
    )

    weighted_one = grad_normed_one * gain_one
    grad_gain_one = jnp.sum(grad_normed_one * inputs * scale_one, axis=0)
    grad_tokens = (
        grad_middle
        + scale_one * weighted_one
        - inputs * scale_one**3 * jnp.mean(weighted_one * inputs, axis=1, keepdims=True)
    )
    packed = jnp.concatenate(
        [
            grad_gain_one,
            grad_gain_two,
            grad_router.reshape(-1),
            table_term.reshape(-1),
        ]
    ).reshape(-1, 128)
    packed = lax.psum(packed, ("fsdp", "ctx", "tp")).reshape(-1)
    gains = packed[: (2 + experts) * width].reshape(2 + experts, width)
    gains = lax.dynamic_slice_in_dim(gains, fsdp_index * own_width, own_width, 1)
    table_grad = packed[(2 + experts) * width :].reshape(heads, BUCKETS)
    return (
        output,
        grad_tokens[None],
        gains[0],
        grad_weight_qkv,
        grad_weight_proj,
        table_grad,
        gains[1],
        gains[2:].T,
        grad_up,
        grad_down,
    )


def solution(mesh):
    rows = P(("fsdp", "tp"), "ctx", None)
    in_specs = (
        rows,
        P(("fsdp", "tp"), None),
        rows,
        P("fsdp"),
        P("fsdp", None),
        P(None, "fsdp"),
        P(),
        P("fsdp"),
        P("fsdp", None),
        P(None, "fsdp", ("ctx", "tp")),
        P(None, ("ctx", "tp"), "fsdp"),
        rows,
    )
    out_specs = (
        rows,
        rows,
        P("fsdp"),
        P("fsdp", None),
        P(None, "fsdp"),
        P(),
        P("fsdp"),
        P("fsdp", None),
        P(None, "fsdp", ("ctx", "tp")),
        P(None, ("ctx", "tp"), "fsdp"),
    )
    return jax.shard_map(local, mesh=mesh, in_specs=in_specs, out_specs=out_specs, check_vma=False)
```

```python
import jax
import jax.numpy as jnp
import numpy as np
from jax import lax
from jax.sharding import PartitionSpec as P

BUCKETS = 32
MAX_DISTANCE = 128
EPSILON = 1e-06
MASK_FILL = -1e30
F32 = jnp.float32
BF16 = jnp.bfloat16


def bucket_bounds(buckets, far_reach):
    exact_count = buckets // 2
    bounds = []
    for number in range(1, buckets):
        if number <= exact_count:
            bounds.append(number)
        else:
            exponent = (number - exact_count) / (buckets - exact_count)
            bounds.append(int(np.ceil(exact_count * (far_reach / exact_count) ** exponent)))
    return bounds


BOUNDS = bucket_bounds(BUCKETS, MAX_DISTANCE)


def rms_scale(values):
    return lax.rsqrt(jnp.mean(values * values, axis=-1, keepdims=True) + EPSILON)


def dot(a, b, ca, cb):
    return lax.dot_general(a, b, (((ca,), (cb,)), ((), ())), preferred_element_type=F32)


def gather(shard, axis, dim):
    count = lax.axis_size(axis)
    size = shard.shape[dim]
    me = lax.axis_index(axis)
    pieces = [shard] + [
        lax.ppermute(shard, axis, [(i, (i + step) % count) for i in range(count)])
        for step in range(1, count)
    ]
    if count == 2:
        first = me == 0
        return jnp.concatenate(
            [jnp.where(first, pieces[0], pieces[1]), jnp.where(first, pieces[1], pieces[0])],
            axis=dim,
        )
    shape = list(shard.shape)
    shape[dim] = count * size
    whole = jnp.zeros(shape, shard.dtype)
    for step, piece in enumerate(pieces):
        source = lax.rem(me + count - step, count)
        whole = lax.dynamic_update_slice_in_dim(whole, piece, source * size, dim)
    return whole


def halving_sum(part, axis):
    count = lax.axis_size(axis)
    me = lax.axis_index(axis)
    bit = 1
    while bit < count:
        mine = lax.rem(me // bit, 2)
        split = part.reshape((part.shape[0] // 2, 2) + part.shape[1:])
        keep = lax.dynamic_index_in_dim(split, mine, 1, keepdims=False)
        send = lax.dynamic_index_in_dim(split, 1 - mine, 1, keepdims=False).astype(BF16)
        got = lax.ppermute(send, axis, [(i, i ^ bit) for i in range(count)])
        part = keep.astype(F32) + got.astype(F32)
        bit *= 2
    return part[0]


def exchange_sum(part, axis, dim, kind=BF16):
    count = lax.axis_size(axis)
    size = part.shape[dim] // count
    me = lax.axis_index(axis)
    total = lax.dynamic_slice_in_dim(part, me * size, size, dim).astype(F32)
    for step in range(1, count):
        target = lax.rem(me + step, count)
        piece = lax.dynamic_slice_in_dim(part, target * size, size, dim).astype(kind)
        total = total + lax.ppermute(
            piece, axis, [(i, (i + step) % count) for i in range(count)]
        ).astype(F32)
    return total


def local(
    tokens,
    seg_ids,
    routes,
    norm_attn,
    weight_qkv,
    weight_proj,
    rel_table,
    norm_ffn,
    weight_router,
    expert_up,
    expert_down,
    cotangent,
):
    rows = tokens.shape[1]
    width = tokens.shape[2]
    heads = rel_table.shape[0]
    head_size = width // heads
    ctx_count = lax.axis_size("ctx")
    heads_here = heads // ctx_count
    hw = heads_here * head_size
    experts = expert_up.shape[0]
    units = expert_up.shape[2]
    length = seg_ids.shape[1]
    score_scale = head_size ** (-0.5)
    ctx_index = lax.axis_index("ctx")
    fsdp_index = lax.axis_index("fsdp")
    own_width = norm_attn.shape[0]
    world = ("ctx", "tp")

    token_group = lax.all_gather(tokens[0], "ctx", axis=0, tiled=True)
    small = jnp.concatenate([norm_attn[None], norm_ffn[None], weight_router.T], axis=0)
    small = gather(small, "fsdp", 1)
    gain_one = small[0].astype(F32)
    gain_two = small[1].astype(F32)
    router_t = small[2:]
    qkv_part = jnp.concatenate(
        [
            lax.dynamic_slice_in_dim(weight_qkv, s * width + ctx_index * hw, hw, 1)
            for s in range(3)
        ],
        axis=1,
    )
    qkv_here = gather(qkv_part, "fsdp", 0)
    proj_full = gather(weight_proj, "fsdp", 1)
    up_t = gather(
        jnp.swapaxes(expert_up, 1, 2).reshape(experts * units, own_width), "fsdp", 1
    )
    down = gather(expert_down.reshape(experts * units, own_width), "fsdp", 1)
    packed_grad = jnp.concatenate(
        [cotangent[0], jnp.pad(routes[0].astype(BF16), ((0, 0), (0, 126)))], axis=1
    )
    grad_routes = lax.all_gather(packed_grad, world, axis=0, tiled=True)

    block = MAX_DISTANCE
    table_here = lax.dynamic_slice_in_dim(rel_table, ctx_index * heads_here, heads_here, 0)
    offset = (
        lax.broadcasted_iota(jnp.int32, (1, block, block), 1)
        - lax.broadcasted_iota(jnp.int32, (1, block, block), 2)
    )

    def bias_block(distance):
        value = jnp.broadcast_to(table_here[:, 0][:, None, None], (heads_here, block, block))
        for number, bound in enumerate(BOUNDS, 1):
            value = jnp.where(distance >= bound, table_here[:, number][:, None, None], value)
        return value

    near = bias_block(offset)
    next_near = bias_block(offset + block)
    far = jnp.broadcast_to(table_here[:, BUCKETS - 1][:, None, None], (heads_here, block, block))
    blocks = length // block
    picks = {0: near, 1: next_near}
    bias = jnp.concatenate(
        [
            jnp.concatenate(
                [picks.get(i - j, far) for j in range(blocks)],
                axis=2,
            )
            for i in range(blocks)
        ],
        axis=1,
    )
    positions = jnp.arange(length, dtype=jnp.int32)
    segment = seg_ids[0]
    allowed = (segment[:, None] == segment[None, :]) & (positions[:, None] >= positions[None, :])
    bias = jnp.where(allowed[None], bias, MASK_FILL)

    inputs_group = token_group.astype(F32)
    normed_group = (inputs_group * rms_scale(inputs_group) * gain_one).astype(BF16)
    projected = dot(normed_group, qkv_here, 1, 0).astype(BF16)
    by_head = projected.reshape(length, 3, heads_here, head_size)
    query, key, value = by_head[:, 0], by_head[:, 1], by_head[:, 2]

    scores = (
        jnp.einsum("qhd,khd->hqk", query, key, preferred_element_type=F32) * score_scale + bias
    )
    peak = jnp.max(scores, axis=-1, keepdims=True)
    weights = jnp.exp(scores - peak)
    probs = weights / jnp.sum(weights, axis=-1, keepdims=True)
    low_probs = probs.astype(BF16)
    attended = (
        jnp.einsum("hqk,khd->qhd", low_probs, value, preferred_element_type=F32)
        .astype(BF16)
        .reshape(length, hw)
    )
    mixed = lax.all_to_all(attended, "ctx", split_axis=0, concat_axis=1, tiled=True)
    inputs = tokens[0].astype(F32)
    scale_one = rms_scale(inputs)
    mixed, grad_routes, up_t, down = lax.optimization_barrier((mixed, grad_routes, up_t, down))
    grad_all = grad_routes[:, :width]
    route_all = grad_routes[:, width : width + 2].astype(jnp.int32)
    middle = inputs + dot(mixed, proj_full, 1, 0)
    scale_two = rms_scale(middle)
    normed_two = (middle * scale_two * gain_two).astype(BF16)

    normed_all = lax.all_gather(normed_two, world, axis=0, tiled=True)

    def gates_of(normed, route):
        logits = dot(normed, router_t, 1, 1)
        number = lax.broadcasted_iota(jnp.int32, (1, experts), 1)
        chosen = (route[:, 0:1] == number) | (route[:, 1:2] == number)
        masked = jnp.where(chosen, logits, MASK_FILL)
        raw = jnp.where(chosen, jnp.exp(masked - jnp.max(masked, axis=1, keepdims=True)), 0.0)
        return raw / jnp.sum(raw, axis=1, keepdims=True)

    gates_all = gates_of(normed_all, route_all)
    column = lax.broadcasted_iota(jnp.int32, (1, experts * units), 1) // units
    spread = gates_all[:, 0:1]
    for e in range(1, experts):
        spread = jnp.where(column >= e, gates_all[:, e : e + 1], spread)
    pre = dot(normed_all, up_t, 1, 1)
    reach = dot(grad_all, down, 1, 1)
    act, gelu_back = jax.vjp(jax.nn.gelu, pre)
    act = act.astype(BF16).astype(F32)
    gated = (act * spread).astype(BF16)
    product = act * reach
    dots_all = jnp.stack(
        [
            jnp.sum(jnp.where(column == e, product, 0.0), axis=1)
            for e in range(experts)
        ],
        axis=0,
    )
    grad_pre = gelu_back(reach * spread)[0].astype(BF16)
    total_rows = normed_all.shape[0]
    devices = total_rows // rows
    tp_count = devices // ctx_count
    dots_all = jnp.swapaxes(dots_all.reshape(experts, devices, rows), 0, 1)
    dots_own = exchange_sum(dots_all.reshape(devices, experts * rows), "ctx", 0, F32)
    dots_own = exchange_sum(dots_own, "tp", 0, F32)
    gate_dots = dots_own.reshape(experts, rows).T
    back = dot(grad_pre, up_t, 1, 0).astype(BF16).reshape(ctx_count, tp_count * rows, width)
    half = width // 2
    grad_normed_two = jnp.concatenate(
        [
            exchange_sum(halving_sum(back[:, :, h * half : (h + 1) * half], "ctx"), "tp", 0)
            for h in range(2)
        ],
        axis=1,
    )
    forth = dot(gated, down, 1, 0).astype(BF16)
    grad_up = exchange_sum(dot(grad_pre, normed_all, 0, 0), "fsdp", 1)
    grad_up = jnp.swapaxes(grad_up.reshape(experts, units, own_width), 1, 2)
    grad_down = exchange_sum(dot(gated, grad_all, 0, 0), "fsdp", 1)
    grad_down = grad_down.reshape(experts, units, own_width)

    grad_out = cotangent[0].astype(F32)
    gates = gates_of(normed_two, routes[0])
    grad_logits = gates * (gate_dots - jnp.sum(gates * gate_dots, axis=1, keepdims=True))
    grad_normed_two = grad_normed_two + jnp.dot(
        grad_logits, router_t.astype(F32), precision=lax.Precision.HIGHEST
    )
    grad_router = lax.dot_general(
        grad_logits,
        normed_two.astype(F32),
        (((0,), (0,)), ((), ())),
        precision=lax.Precision.HIGHEST,
    )
    weighted_two = grad_normed_two * gain_two
    grad_gain_two = jnp.sum(grad_normed_two * middle * scale_two, axis=0)
    grad_middle = (
        grad_out
        + scale_two * weighted_two
        - middle * scale_two**3 * jnp.mean(weighted_two * middle, axis=1, keepdims=True)
    )
    grad_mid_group = lax.all_gather(grad_middle.astype(BF16), "ctx", axis=0, tiled=True)
    forth, grad_mid_group = lax.optimization_barrier((forth, grad_mid_group))
    result = lax.psum_scatter(forth, world, scatter_dimension=0, tiled=True)

    proj_rows = lax.dynamic_slice_in_dim(proj_full, ctx_index * hw, hw, 0)
    grad_attended = dot(grad_mid_group, proj_rows, 1, 1).astype(BF16)
    grad_heads = grad_attended.reshape(length, heads_here, head_size)
    grad_value = jnp.einsum("hqk,qhd->khd", low_probs, grad_heads, preferred_element_type=F32)
    grad_probs = jnp.einsum("qhd,khd->hqk", grad_heads, value, preferred_element_type=F32)
    grad_scores = (
        probs * (grad_probs - jnp.sum(probs * grad_probs, axis=-1, keepdims=True))
    ).astype(BF16)
    grad_query = (
        jnp.einsum("hqk,khd->qhd", grad_scores, key, preferred_element_type=F32) * score_scale
    )
    grad_key = (
        jnp.einsum("hqk,qhd->khd", grad_scores, query, preferred_element_type=F32) * score_scale
    )
    grad_qkv = jnp.concatenate(
        [
            grad_query.astype(BF16).reshape(length, hw),
            grad_key.astype(BF16).reshape(length, hw),
            grad_value.astype(BF16).reshape(length, hw),
        ],
        axis=1,
    )
    grad_normed_one = exchange_sum(dot(grad_qkv, qkv_here, 1, 1), "ctx", 0)

    weight_part = jnp.concatenate(
        [dot(normed_group, grad_qkv, 0, 0), dot(grad_mid_group, attended, 0, 0)], axis=1
    )
    weight_own = exchange_sum(weight_part, "fsdp", 0)
    weight_own = exchange_sum(weight_own, "tp", 0).astype(BF16)
    def score_block(i, j):
        return grad_scores[
            :, i * block : (i + 1) * block, j * block : (j + 1) * block
        ].astype(F32)

    near_sum = sum(score_block(i, i) for i in range(blocks))
    next_sum = sum(score_block(i + 1, i) for i in range(blocks - 1))
    far_sum = sum(
        jnp.sum(score_block(i, j), axis=(1, 2)) for i in range(blocks) for j in range(i - 1)
    )
    lows = [0] + BOUNDS
    highs = BOUNDS + [2 * block]
    bucket_sums = [
        jnp.sum(jnp.where((offset >= lo) & (offset < hi), near_sum, 0.0), axis=(1, 2))
        + jnp.sum(
            jnp.where((offset + block >= lo) & (offset + block < hi), next_sum, 0.0), axis=(1, 2)
        )
        for lo, hi in zip(lows, highs)
    ]
    bucket_sums[-1] = bucket_sums[-1] + far_sum
    table_here_grad = jnp.stack(bucket_sums, axis=1)
    table_term = lax.dynamic_update_slice_in_dim(
        jnp.zeros((heads, BUCKETS), F32), table_here_grad, ctx_index * heads_here, 0
    )

    weighted_one = grad_normed_one * gain_one
    grad_gain_one = jnp.sum(grad_normed_one * inputs * scale_one, axis=0)
    grad_tokens = (
        grad_middle
        + scale_one * weighted_one
        - inputs * scale_one**3 * jnp.mean(weighted_one * inputs, axis=1, keepdims=True)
    )
    packed = jnp.concatenate(
        [
            grad_gain_one,
            grad_gain_two,
            grad_router.reshape(-1),
            table_term.reshape(-1),
        ]
    ).reshape(-1, 128)
    packed, weight_own = lax.optimization_barrier((packed, weight_own))
    packed = lax.psum(packed, ("fsdp", "ctx", "tp")).reshape(-1)
    packed, result = lax.optimization_barrier((packed, result))
    output = (middle + result.astype(F32)).astype(BF16)[None]
    weight_all = lax.all_gather(weight_own, world, axis=0, tiled=True).astype(F32)
    weight_all = weight_all.reshape(ctx_count, own_width, 4 * hw)
    grad_weight_qkv = jnp.concatenate(
        [
            weight_all[c, :, s * hw : (s + 1) * hw]
            for s in range(3)
            for c in range(ctx_count)
        ],
        axis=1,
    )
    grad_weight_proj = jnp.swapaxes(weight_all[:, :, 3 * hw :], 1, 2).reshape(width, own_width)
    gains = packed[: (2 + experts) * width].reshape(2 + experts, width)
    gains = lax.dynamic_slice_in_dim(gains, fsdp_index * own_width, own_width, 1)
    table_grad = packed[(2 + experts) * width :].reshape(heads, BUCKETS)
    return (
        output,
        grad_tokens[None],
        gains[0],
        grad_weight_qkv,
        grad_weight_proj,
        table_grad,
        gains[1],
        gains[2:].T,
        grad_up,
        grad_down,
    )


def solution(mesh):
    rows = P(("fsdp", "tp"), "ctx", None)
    in_specs = (
        rows,
        P(("fsdp", "tp"), None),
        rows,
        P("fsdp"),
        P("fsdp", None),
        P(None, "fsdp"),
        P(),
        P("fsdp"),
        P("fsdp", None),
        P(None, "fsdp", ("ctx", "tp")),
        P(None, ("ctx", "tp"), "fsdp"),
        rows,
    )
    out_specs = (
        rows,
        rows,
        P("fsdp"),
        P("fsdp", None),
        P(None, "fsdp"),
        P(),
        P("fsdp"),
        P("fsdp", None),
        P(None, "fsdp", ("ctx", "tp")),
        P(None, ("ctx", "tp"), "fsdp"),
    )
    return jax.shard_map(local, mesh=mesh, in_specs=in_specs, out_specs=out_specs, check_vma=False)
```

```python
import jax
import jax.numpy as jnp
import numpy as np
from jax import lax
from jax.sharding import PartitionSpec as P

BUCKETS = 32
MAX_DISTANCE = 128
EPSILON = 1e-06
MASK_FILL = -1e30
F32 = jnp.float32
BF16 = jnp.bfloat16


def bucket_bounds(buckets, far_reach):
    exact_count = buckets // 2
    bounds = []
    for number in range(1, buckets):
        if number <= exact_count:
            bounds.append(number)
        else:
            exponent = (number - exact_count) / (buckets - exact_count)
            bounds.append(int(np.ceil(exact_count * (far_reach / exact_count) ** exponent)))
    return bounds


BOUNDS = bucket_bounds(BUCKETS, MAX_DISTANCE)


def rms_scale(values):
    return lax.rsqrt(jnp.mean(values * values, axis=-1, keepdims=True) + EPSILON)


def dot(a, b, ca, cb):
    return lax.dot_general(a, b, (((ca,), (cb,)), ((), ())), preferred_element_type=F32)


def gather(shard, axis, dim):
    count = lax.axis_size(axis)
    size = shard.shape[dim]
    me = lax.axis_index(axis)
    pieces = [shard] + [
        lax.ppermute(shard, axis, [(i, (i + step) % count) for i in range(count)])
        for step in range(1, count)
    ]
    if count == 2:
        first = me == 0
        return jnp.concatenate(
            [jnp.where(first, pieces[0], pieces[1]), jnp.where(first, pieces[1], pieces[0])],
            axis=dim,
        )
    shape = list(shard.shape)
    shape[dim] = count * size
    whole = jnp.zeros(shape, shard.dtype)
    for step, piece in enumerate(pieces):
        source = lax.rem(me + count - step, count)
        whole = lax.dynamic_update_slice_in_dim(whole, piece, source * size, dim)
    return whole


def halving_sum(part, axis):
    count = lax.axis_size(axis)
    me = lax.axis_index(axis)
    bit = 1
    while bit < count:
        mine = lax.rem(me // bit, 2)
        split = part.reshape((part.shape[0] // 2, 2) + part.shape[1:])
        keep = lax.dynamic_index_in_dim(split, mine, 1, keepdims=False)
        send = lax.dynamic_index_in_dim(split, 1 - mine, 1, keepdims=False).astype(BF16)
        got = lax.ppermute(send, axis, [(i, i ^ bit) for i in range(count)])
        part = keep.astype(F32) + got.astype(F32)
        bit *= 2
    return part[0]


def exchange_sum(part, axis, dim, kind=BF16):
    count = lax.axis_size(axis)
    size = part.shape[dim] // count
    me = lax.axis_index(axis)
    total = lax.dynamic_slice_in_dim(part, me * size, size, dim).astype(F32)
    for step in range(1, count):
        target = lax.rem(me + step, count)
        piece = lax.dynamic_slice_in_dim(part, target * size, size, dim).astype(kind)
        total = total + lax.ppermute(
            piece, axis, [(i, (i + step) % count) for i in range(count)]
        ).astype(F32)
    return total


def local(
    tokens,
    seg_ids,
    routes,
    norm_attn,
    weight_qkv,
    weight_proj,
    rel_table,
    norm_ffn,
    weight_router,
    expert_up,
    expert_down,
    cotangent,
):
    rows = tokens.shape[1]
    width = tokens.shape[2]
    heads = rel_table.shape[0]
    head_size = width // heads
    ctx_count = lax.axis_size("ctx")
    heads_here = heads // ctx_count
    hw = heads_here * head_size
    experts = expert_up.shape[0]
    units = expert_up.shape[2]
    length = seg_ids.shape[1]
    score_scale = head_size ** (-0.5)
    ctx_index = lax.axis_index("ctx")
    fsdp_index = lax.axis_index("fsdp")
    own_width = norm_attn.shape[0]
    world = ("ctx", "tp")

    token_group = lax.all_gather(tokens[0], "ctx", axis=0, tiled=True)
    small = jnp.concatenate([norm_attn[None], norm_ffn[None], weight_router.T], axis=0)
    small = gather(small, "fsdp", 1)
    gain_one = small[0].astype(F32)
    gain_two = small[1].astype(F32)
    router_t = small[2:]
    qkv_part = jnp.concatenate(
        [
            lax.dynamic_slice_in_dim(weight_qkv, s * width + ctx_index * hw, hw, 1)
            for s in range(3)
        ],
        axis=1,
    )
    qkv_here = gather(qkv_part, "fsdp", 0)
    proj_full = gather(weight_proj, "fsdp", 1)
    up_t = gather(
        jnp.swapaxes(expert_up, 1, 2).reshape(experts * units, own_width), "fsdp", 1
    )
    down = gather(expert_down.reshape(experts * units, own_width), "fsdp", 1)
    packed_grad = jnp.concatenate(
        [cotangent[0], jnp.pad(routes[0].astype(BF16), ((0, 0), (0, 126)))], axis=1
    )
    grad_routes = lax.all_gather(packed_grad, world, axis=0, tiled=True)

    block = MAX_DISTANCE
    table_here = lax.dynamic_slice_in_dim(rel_table, ctx_index * heads_here, heads_here, 0)
    offset = (
        lax.broadcasted_iota(jnp.int32, (1, block, block), 1)
        - lax.broadcasted_iota(jnp.int32, (1, block, block), 2)
    )

    def bias_block(distance):
        value = jnp.broadcast_to(table_here[:, 0][:, None, None], (heads_here, block, block))
        for number, bound in enumerate(BOUNDS, 1):
            value = jnp.where(distance >= bound, table_here[:, number][:, None, None], value)
        return value

    near = bias_block(offset)
    next_near = bias_block(offset + block)
    far = jnp.broadcast_to(table_here[:, BUCKETS - 1][:, None, None], (heads_here, block, block))
    blocks = length // block
    picks = {0: near, 1: next_near}
    bias = jnp.concatenate(
        [
            jnp.concatenate(
                [picks.get(i - j, far) for j in range(blocks)],
                axis=2,
            )
            for i in range(blocks)
        ],
        axis=1,
    )
    positions = jnp.arange(length, dtype=jnp.int32)
    segment = seg_ids[0]
    allowed = (segment[:, None] == segment[None, :]) & (positions[:, None] >= positions[None, :])
    bias = jnp.where(allowed[None], bias, MASK_FILL)

    inputs_group = token_group.astype(F32)
    normed_group = (inputs_group * rms_scale(inputs_group) * gain_one).astype(BF16)
    projected = dot(normed_group, qkv_here, 1, 0).astype(BF16)
    by_head = projected.reshape(length, 3, heads_here, head_size)
    query, key, value = by_head[:, 0], by_head[:, 1], by_head[:, 2]

    scores = (
        jnp.einsum("qhd,khd->hqk", query, key, preferred_element_type=F32) * score_scale + bias
    )
    peak = jnp.max(scores, axis=-1, keepdims=True)
    weights = jnp.exp(scores - peak)
    probs = weights / jnp.sum(weights, axis=-1, keepdims=True)
    low_probs = probs.astype(BF16)
    attended = (
        jnp.einsum("hqk,khd->qhd", low_probs, value, preferred_element_type=F32)
        .astype(BF16)
        .reshape(length, hw)
    )
    mixed = lax.all_to_all(attended, "ctx", split_axis=0, concat_axis=1, tiled=True)
    inputs = tokens[0].astype(F32)
    scale_one = rms_scale(inputs)
    mixed, grad_routes, up_t, down = lax.optimization_barrier((mixed, grad_routes, up_t, down))
    grad_all = grad_routes[:, :width]
    route_all = grad_routes[:, width : width + 2].astype(jnp.int32)
    middle = inputs + dot(mixed, proj_full, 1, 0)
    scale_two = rms_scale(middle)
    normed_two = (middle * scale_two * gain_two).astype(BF16)

    normed_all = lax.all_gather(normed_two, world, axis=0, tiled=True)

    def gates_of(normed, route):
        logits = dot(normed, router_t, 1, 1)
        number = lax.broadcasted_iota(jnp.int32, (1, experts), 1)
        chosen = (route[:, 0:1] == number) | (route[:, 1:2] == number)
        masked = jnp.where(chosen, logits, MASK_FILL)
        raw = jnp.where(chosen, jnp.exp(masked - jnp.max(masked, axis=1, keepdims=True)), 0.0)
        return raw / jnp.sum(raw, axis=1, keepdims=True)

    gates_all = gates_of(normed_all, route_all)
    column = lax.broadcasted_iota(jnp.int32, (1, experts * units), 1) // units
    spread = gates_all[:, 0:1]
    for e in range(1, experts):
        spread = jnp.where(column >= e, gates_all[:, e : e + 1], spread)
    pre = dot(normed_all, up_t, 1, 1)
    reach = dot(grad_all, down, 1, 1)
    act, gelu_back = jax.vjp(jax.nn.gelu, pre)
    act = act.astype(BF16).astype(F32)
    gated = (act * spread).astype(BF16)
    product = act * reach
    dots_all = jnp.stack(
        [
            jnp.sum(jnp.where(column == e, product, 0.0), axis=1)
            for e in range(experts)
        ],
        axis=0,
    )
    grad_pre = gelu_back(reach * spread)[0].astype(BF16)
    total_rows = normed_all.shape[0]
    devices = total_rows // rows
    tp_count = devices // ctx_count
    dots_all = jnp.swapaxes(dots_all.reshape(experts, devices, rows), 0, 1)
    dots_own = exchange_sum(dots_all.reshape(devices, experts * rows), "ctx", 0, F32)
    dots_own = exchange_sum(dots_own, "tp", 0, F32)
    gate_dots = dots_own.reshape(experts, rows).T
    back = dot(grad_pre, up_t, 1, 0).astype(BF16).reshape(ctx_count, tp_count * rows, width)
    half = width // 2
    grad_normed_two = jnp.concatenate(
        [
            exchange_sum(halving_sum(back[:, :, h * half : (h + 1) * half], "ctx"), "tp", 0)
            for h in range(2)
        ],
        axis=1,
    )
    forth = dot(gated, down, 1, 0).astype(BF16)
    grad_up = exchange_sum(dot(grad_pre, normed_all, 0, 0), "fsdp", 1)
    grad_up = jnp.swapaxes(grad_up.reshape(experts, units, own_width), 1, 2)
    grad_down = exchange_sum(dot(gated, grad_all, 0, 0), "fsdp", 1)
    grad_down = grad_down.reshape(experts, units, own_width)

    grad_out = cotangent[0].astype(F32)
    gates = gates_of(normed_two, routes[0])
    grad_logits = gates * (gate_dots - jnp.sum(gates * gate_dots, axis=1, keepdims=True))
    grad_normed_two = grad_normed_two + jnp.dot(
        grad_logits, router_t.astype(F32), precision=lax.Precision.HIGHEST
    )
    grad_router = lax.dot_general(
        grad_logits,
        normed_two.astype(F32),
        (((0,), (0,)), ((), ())),
        precision=lax.Precision.HIGHEST,
    )
    weighted_two = grad_normed_two * gain_two
    grad_gain_two = jnp.sum(grad_normed_two * middle * scale_two, axis=0)
    grad_middle = (
        grad_out
        + scale_two * weighted_two
        - middle * scale_two**3 * jnp.mean(weighted_two * middle, axis=1, keepdims=True)
    )
    grad_mid_group = lax.all_gather(grad_middle.astype(BF16), "ctx", axis=0, tiled=True)
    forth, grad_mid_group = lax.optimization_barrier((forth, grad_mid_group))
    forth = forth.reshape(ctx_count, tp_count * rows, width)
    result = exchange_sum(halving_sum(forth, "ctx"), "tp", 0)

    proj_rows = lax.dynamic_slice_in_dim(proj_full, ctx_index * hw, hw, 0)
    grad_attended = dot(grad_mid_group, proj_rows, 1, 1).astype(BF16)
    grad_heads = grad_attended.reshape(length, heads_here, head_size)
    grad_value = jnp.einsum("hqk,qhd->khd", low_probs, grad_heads, preferred_element_type=F32)
    grad_probs = jnp.einsum("qhd,khd->hqk", grad_heads, value, preferred_element_type=F32)
    grad_scores = (
        probs * (grad_probs - jnp.sum(probs * grad_probs, axis=-1, keepdims=True))
    ).astype(BF16)
    grad_query = (
        jnp.einsum("hqk,khd->qhd", grad_scores, key, preferred_element_type=F32) * score_scale
    )
    grad_key = (
        jnp.einsum("hqk,qhd->khd", grad_scores, query, preferred_element_type=F32) * score_scale
    )
    grad_qkv = jnp.concatenate(
        [
            grad_query.astype(BF16).reshape(length, hw),
            grad_key.astype(BF16).reshape(length, hw),
            grad_value.astype(BF16).reshape(length, hw),
        ],
        axis=1,
    )
    grad_normed_one = exchange_sum(dot(grad_qkv, qkv_here, 1, 1), "ctx", 0)

    weight_part = jnp.concatenate(
        [dot(normed_group, grad_qkv, 0, 0), dot(grad_mid_group, attended, 0, 0)], axis=1
    )
    weight_own = exchange_sum(weight_part, "fsdp", 0)
    grad_scores, weight_own = lax.optimization_barrier((grad_scores, weight_own))
    weight_own = exchange_sum(weight_own, "tp", 0).astype(BF16)
    def score_block(i, j):
        return grad_scores[
            :, i * block : (i + 1) * block, j * block : (j + 1) * block
        ].astype(F32)

    near_sum = sum(score_block(i, i) for i in range(blocks))
    next_sum = sum(score_block(i + 1, i) for i in range(blocks - 1))
    far_sum = sum(
        jnp.sum(score_block(i, j), axis=(1, 2)) for i in range(blocks) for j in range(i - 1)
    )
    lows = [0] + BOUNDS
    highs = BOUNDS + [2 * block]
    bucket_sums = [
        jnp.sum(jnp.where((offset >= lo) & (offset < hi), near_sum, 0.0), axis=(1, 2))
        + jnp.sum(
            jnp.where((offset + block >= lo) & (offset + block < hi), next_sum, 0.0), axis=(1, 2)
        )
        for lo, hi in zip(lows, highs)
    ]
    bucket_sums[-1] = bucket_sums[-1] + far_sum
    table_here_grad = jnp.stack(bucket_sums, axis=1)
    table_term = lax.dynamic_update_slice_in_dim(
        jnp.zeros((heads, BUCKETS), F32), table_here_grad, ctx_index * heads_here, 0
    )

    weighted_one = grad_normed_one * gain_one
    grad_gain_one = jnp.sum(grad_normed_one * inputs * scale_one, axis=0)
    grad_tokens = (
        grad_middle
        + scale_one * weighted_one
        - inputs * scale_one**3 * jnp.mean(weighted_one * inputs, axis=1, keepdims=True)
    )
    packed = jnp.concatenate(
        [
            grad_gain_one,
            grad_gain_two,
            grad_router.reshape(-1),
            table_term.reshape(-1),
        ]
    ).reshape(-1, 128)
    packed, weight_own = lax.optimization_barrier((packed, weight_own))
    packed = lax.psum(packed, ("fsdp", "ctx", "tp")).reshape(-1)
    packed, result = lax.optimization_barrier((packed, result))
    output = (middle + result).astype(BF16)[None]
    weight_all = lax.all_gather(weight_own, world, axis=0, tiled=True).astype(F32)
    weight_all = weight_all.reshape(ctx_count, own_width, 4 * hw)
    grad_weight_qkv = jnp.concatenate(
        [
            weight_all[c, :, s * hw : (s + 1) * hw]
            for s in range(3)
            for c in range(ctx_count)
        ],
        axis=1,
    )
    grad_weight_proj = jnp.swapaxes(weight_all[:, :, 3 * hw :], 1, 2).reshape(width, own_width)
    gains = packed[: (2 + experts) * width].reshape(2 + experts, width)
    gains = lax.dynamic_slice_in_dim(gains, fsdp_index * own_width, own_width, 1)
    table_grad = packed[(2 + experts) * width :].reshape(heads, BUCKETS)
    return (
        output,
        grad_tokens[None],
        gains[0],
        grad_weight_qkv,
        grad_weight_proj,
        table_grad,
        gains[1],
        gains[2:].T,
        grad_up,
        grad_down,
    )


def solution(mesh):
    rows = P(("fsdp", "tp"), "ctx", None)
    in_specs = (
        rows,
        P(("fsdp", "tp"), None),
        rows,
        P("fsdp"),
        P("fsdp", None),
        P(None, "fsdp"),
        P(),
        P("fsdp"),
        P("fsdp", None),
        P(None, "fsdp", ("ctx", "tp")),
        P(None, ("ctx", "tp"), "fsdp"),
        rows,
    )
    out_specs = (
        rows,
        rows,
        P("fsdp"),
        P("fsdp", None),
        P(None, "fsdp"),
        P(),
        P("fsdp"),
        P("fsdp", None),
        P(None, "fsdp", ("ctx", "tp")),
        P(None, ("ctx", "tp"), "fsdp"),
    )
    return jax.shard_map(local, mesh=mesh, in_specs=in_specs, out_specs=out_specs, check_vma=False)
```
